32 devices in a mesh: dev: 32 (over z, y, x, core).
Axes of the slice: x: 2, y: 2, z: 4, core: 2. Of those that a mesh axis runs over, the one named last changes fastest.
Arguments:
- inputs: bfloat16 [64, 256, 384], P('dev'), may hold values from -6 to 6
- cond: bfloat16 [64, 384], P('dev'), may hold values from -6 to 6
- cotan: bfloat16 [64, 256, 384], P('dev'), may hold values from -6 to 6
- counts: int32 [32], P('dev'), may hold values from 1 to 2, as said below
- w_ada: bfloat16 [884736], P('dev'), may hold values from -0.3125 to 0.3125
- w_qkv: bfloat16 [442368], P('dev'), may hold values from -0.3125 to 0.3125
- w_out: bfloat16 [147456], P('dev'), may hold values from -1.25 to 1.25
- w_up: bfloat16 [589824], P('dev'), may hold values from -0.3125 to 0.3125
- w_down: bfloat16 [589824], P('dev'), may hold values from -0.15625 to 0.15625
- biases: bfloat16 [5376], P('dev'), may hold values from -3 to 3
Outputs:
- output: float32 [64, 256, 384], P('dev')
- grad_inputs: float32 [64, 256, 384], P('dev')
- grad_cond: float32 [64, 384], P('dev')
- grad_ada: float32 [884736], P('dev')
- grad_qkv: float32 [442368], P('dev')
- grad_out: float32 [147456], P('dev')
- grad_up: float32 [589824], P('dev')
- grad_down: float32 [589824], P('dev')
- grad_biases: float32 [5376], P('dev')
The draws below stay inside these ranges and needn't reach their ends.
Inputs may be any that keep to these rules, and one draw needn't show every extreme that they name: `counts`: each device has between 1 and 2 live latents, and some device has exactly 2.
All inputs are finite; a program needn't handle non-finite values.
Results may differ from the reference program's by a relative error of at most 0.009.
The reference program's roundings to bfloat16 on the way count: a program that leaves them out, or rounds other values in their place, can miss the bound.
Values may be sent and summed in bfloat16 or wider, within the bound.
A program may use at most 128 MiB of HBM per device.

```python
import math
import jax
import jax.numpy as jnp
from jax import lax

D = 384
HEADS = 6
FF = 1536
TOK = 256
LAT_DEV = 2
SLOTS = 64
NBIAS = 5376
N_DEV = 32


def draw_counts(key, part):
    first_key, second_key = jax.random.split(jax.random.fold_in(key, 11))
    drawn_counts = jax.random.randint(first_key, (N_DEV,), 1, LAT_DEV + 1)
    chosen_device = jax.random.randint(second_key, (), 0, N_DEV)
    return jnp.where(jnp.arange(N_DEV) == chosen_device, LAT_DEV, drawn_counts).astype(jnp.int32)


def steps_of(own_key, shape, cuts, low, largest):
    def one(axis_at, blocks):
        steps = jax.random.uniform(jax.random.fold_in(jax.random.fold_in(own_key, 6), axis_at), (blocks,), jnp.float32, low / len(cuts), largest / len(cuts))
        return jnp.repeat(jnp.exp(steps), shape[axis_at] // blocks).reshape((-1,) + (1,) * (len(shape) - axis_at - 1))

    gain = one(*cuts[0])
    for cut in cuts[1:]:
        gain = gain * one(*cut)
    return gain


def normal_values(rng, dims, scale, reach, cuts=(), dtype=jnp.bfloat16):
    values = jax.random.normal(rng, dims, jnp.float32) * scale
    if len(cuts) > 0:
        values = steps_of(rng, dims, cuts, -0.22, 0.18) * values
    return jnp.clip(values, min=-reach, max=reach).astype(dtype)


def setup_inputs(seed: int = 0) -> dict:
    key_list = jax.random.split(jax.random.key(seed), 11)
    inputs = normal_values(key_list[0], (SLOTS, TOK, D), 1.0, 6.0, ((0, 32),))
    cond = normal_values(key_list[1], (SLOTS, D), 1.0, 6.0, ((0, 32),))
    cotan = normal_values(key_list[2], (SLOTS, TOK, D), 1.0, 6.0, ((0, 32),))
    counts = draw_counts(jax.random.fold_in(key_list[10], 71), 0)
    w_ada = normal_values(key_list[4], (6 * D * D,), D ** -0.5, 0.3125, ((0, 32),))
    w_qkv = normal_values(key_list[5], (3 * D * D,), D ** -0.5, 0.3125, ((0, 32),))
    w_out = normal_values(key_list[6], (D * D,), (D // 16) ** -0.5, 1.25, ((0, 32),))
    w_up = normal_values(key_list[7], (D * FF,), D ** -0.5, 0.3125, ((0, 32),))
    w_down = normal_values(key_list[8], (FF * D,), FF ** -0.5, 0.15625, ((0, 32),))
    biases = normal_values(key_list[9], (NBIAS,), 0.5, 3.0, ((0, 32),))
    return {"inputs": inputs, "cond": cond, "cotan": cotan, "counts": counts, "w_ada": w_ada, "w_qkv": w_qkv, "w_out": w_out, "w_up": w_up, "w_down": w_down, "biases": biases}


EPS = 1e-06
GELU_C = 0.7978845608028654

def apply_gelu(pre):
    return 0.5 * pre * (1.0 + jnp.tanh(GELU_C * (pre + 0.044715 * pre * pre * pre)))

def gelu_slope(pre):
    tangent = jnp.tanh(GELU_C * (pre + 0.044715 * pre * pre * pre))
    return 0.5 * (1.0 + tangent) + 0.5 * pre * (1.0 - tangent * tangent) * GELU_C * (1.0 + 3.0 * 0.044715 * pre * pre)

def layer_norm(field):
    centred = field - lax.optimization_barrier(jnp.mean(field, axis=-1, keepdims=True))
    inv_dev = lax.rsqrt(lax.optimization_barrier(jnp.mean(centred * centred, axis=-1, keepdims=True)) + EPS)
    return (centred * inv_dev, inv_dev)

def norm_backward(grad_h, normed, inv_dev):
    return inv_dev * (grad_h - lax.optimization_barrier(jnp.mean(grad_h, axis=-1, keepdims=True)) - normed * lax.optimization_barrier(jnp.mean(grad_h * normed, axis=-1, keepdims=True)))

def flat_dot(left, right):
    result = jnp.dot(left.reshape(-1, left.shape[-1]), right, preferred_element_type=jnp.float32)
    return result.reshape(left.shape[:-1] + (right.shape[-1],))

def back_dot(left, right):
    result = jnp.dot(left.reshape(-1, left.shape[-1]), right.T, preferred_element_type=jnp.float32)
    return result.reshape(left.shape[:-1] + (right.shape[0],))

def grad_dot(left, right):
    return lax.dot_general(left.reshape(-1, left.shape[-1]), right.reshape(-1, right.shape[-1]), (((0,), (0,)), ((), ())), preferred_element_type=jnp.float32)

def batched(form, left, right):
    return jnp.einsum(form, left.astype(jnp.float32), right.astype(jnp.float32))

def split_bias(bias_all, width, hidden_units):
    bias_f = bias_all.astype(jnp.float32)
    return (bias_f[:6 * width], bias_f[6 * width:7 * width], bias_f[7 * width:8 * width], bias_f[8 * width:9 * width], bias_f[9 * width:9 * width + hidden_units], bias_f[9 * width + hidden_units:])

def device_forward(inputs, cond, live, mats):
    w_ada, w_qkv, w_out, w_up, w_down, bias_all = mats
    latents, tokens, width = inputs.shape
    hidden_units = w_up.shape[1]
    head_size = width // HEADS
    b_ada, b_query, b_value, b_out, b_up, b_down = split_bias(bias_all, width, hidden_units)
    cond_f = cond.astype(jnp.float32)
    cond_act = (cond_f * jax.nn.sigmoid(cond_f)).astype(jnp.bfloat16)
    modul = jnp.dot(cond_act, w_ada, preferred_element_type=jnp.float32) + b_ada
    pieces = [modul[:, None, index * width:(index + 1) * width] for index in range(6)]
    shift_one, scale_one, gate_one, shift_two, scale_two, gate_two = pieces
    resid = inputs.astype(jnp.float32)
    normed_one, inv_one = layer_norm(resid)
    mod_one = (normed_one * (1.0 + scale_one) + shift_one).astype(jnp.bfloat16)
    proj = flat_dot(mod_one, w_qkv)
    split_shape = (latents, tokens, HEADS, head_size)
    queries = (proj[..., :width] + b_query).astype(jnp.bfloat16).reshape(split_shape)
    keys_bf = proj[..., width:2 * width].astype(jnp.bfloat16).reshape(split_shape)
    values_bf = (proj[..., 2 * width:] + b_value).astype(jnp.bfloat16).reshape(split_shape)
    factor = 1.0 / math.sqrt(head_size)
    scores = batched('lqhe,lkhe->lhqk', queries, keys_bf) * factor
    highest = lax.optimization_barrier(jnp.max(scores, axis=-1, keepdims=True))
    expd = jnp.exp(scores - highest)
    totals = lax.optimization_barrier(jnp.sum(expd, axis=-1, keepdims=True))
    probs = (expd / totals).astype(jnp.bfloat16)
    log_total = highest + jnp.log(totals)
    attended = batched('lhqk,lkhe->lqhe', probs, values_bf).astype(jnp.bfloat16).reshape(latents, tokens, width)
    att_out = flat_dot(attended, w_out) + b_out
    resid_one = resid + gate_one * att_out
    normed_two, inv_two = layer_norm(resid_one)
    mod_two = (normed_two * (1.0 + scale_two) + shift_two).astype(jnp.bfloat16)
    pre_act = flat_dot(mod_two, w_up) + b_up
    activ = apply_gelu(pre_act).astype(jnp.bfloat16)
    mlp_out = flat_dot(activ, w_down) + b_down
    output = (resid_one + gate_two * mlp_out) * live[:, None, None]
    saved = dict(cond_f=cond_f, cond_act=cond_act, scale_one=scale_one, gate_one=gate_one, scale_two=scale_two, gate_two=gate_two, normed_one=normed_one, inv_one=inv_one, mod_one=mod_one, queries=queries, keys_bf=keys_bf, values_bf=values_bf, log_total=log_total, attended=attended, att_out=att_out, normed_two=normed_two, inv_two=inv_two, mod_two=mod_two, pre_act=pre_act, activ=activ, mlp_out=mlp_out)
    return (output, saved)

def device_backward(cotan, live, mats, saved):
    w_ada, w_qkv, w_out, w_up, w_down, bias_all = mats
    latents, tokens, width = cotan.shape
    head_size = width // HEADS
    factor = 1.0 / math.sqrt(head_size)
    grad_y = cotan.astype(jnp.float32) * live[:, None, None]
    g_gate_two = lax.optimization_barrier(jnp.sum(grad_y * saved['mlp_out'], axis=1))
    g_mlp = grad_y * saved['gate_two']
    g_mlp_b = g_mlp.astype(jnp.bfloat16)
    gw_down = grad_dot(saved['activ'], g_mlp_b)
    gb_down = lax.optimization_barrier(jnp.sum(g_mlp, axis=(0, 1)))
    g_pre = back_dot(g_mlp_b, w_down) * gelu_slope(saved['pre_act'])
    g_pre_b = g_pre.astype(jnp.bfloat16)
    gw_up = grad_dot(saved['mod_two'], g_pre_b)
    gb_up = lax.optimization_barrier(jnp.sum(g_pre, axis=(0, 1)))
    g_mod_two = back_dot(g_pre_b, w_up)
    g_scale_two = lax.optimization_barrier(jnp.sum(g_mod_two * saved['normed_two'], axis=1))
    g_shift_two = lax.optimization_barrier(jnp.sum(g_mod_two, axis=1))
    g_resid_one = grad_y + norm_backward(g_mod_two * (1.0 + saved['scale_two']), saved['normed_two'], saved['inv_two'])
    g_gate_one = lax.optimization_barrier(jnp.sum(g_resid_one * saved['att_out'], axis=1))
    g_attn = g_resid_one * saved['gate_one']
    g_attn_b = g_attn.astype(jnp.bfloat16)
    gw_out = grad_dot(saved['attended'], g_attn_b)
    gb_out = lax.optimization_barrier(jnp.sum(g_attn, axis=(0, 1)))
    split_shape = (latents, tokens, HEADS, head_size)
    g_attended = back_dot(g_attn_b, w_out).astype(jnp.bfloat16).reshape(split_shape)
    queries, keys_bf, values_bf = (saved['queries'], saved['keys_bf'], saved['values_bf'])
    scores = batched('lqhe,lkhe->lhqk', queries, keys_bf) * factor
    probs_f = jnp.exp(scores - saved['log_total'])
    probs_b = probs_f.astype(jnp.bfloat16)
    g_values = batched('lhqk,lqhe->lkhe', probs_b, g_attended)
    g_probs = batched('lqhe,lkhe->lhqk', g_attended, values_bf)
    row_dot = lax.optimization_barrier(jnp.sum(g_attended.astype(jnp.float32) * saved['attended'].astype(jnp.float32).reshape(split_shape), axis=-1))
    row_dot = jnp.transpose(row_dot, (0, 2, 1))[..., None]
    g_scores = (probs_f * (g_probs - row_dot) * factor).astype(jnp.bfloat16)
    g_query = batched('lhqk,lkhe->lqhe', g_scores, keys_bf).reshape(latents, tokens, width)
    g_key = batched('lhqk,lqhe->lkhe', g_scores, queries).reshape(latents, tokens, width)
    g_values = g_values.reshape(latents, tokens, width)
    g_proj_b = jnp.concatenate([g_query, g_key, g_values], axis=-1).astype(jnp.bfloat16)
    gw_qkv = grad_dot(saved['mod_one'], g_proj_b)
    gb_query = lax.optimization_barrier(jnp.sum(g_query, axis=(0, 1)))
    gb_value = lax.optimization_barrier(jnp.sum(g_values, axis=(0, 1)))
    g_mod_one = back_dot(g_proj_b, w_qkv)
    g_scale_one = lax.optimization_barrier(jnp.sum(g_mod_one * saved['normed_one'], axis=1))
    g_shift_one = lax.optimization_barrier(jnp.sum(g_mod_one, axis=1))
    g_inputs = g_resid_one + norm_backward(g_mod_one * (1.0 + saved['scale_one']), saved['normed_one'], saved['inv_one'])
    g_modul = jnp.concatenate([g_shift_one, g_scale_one, g_gate_one, g_shift_two, g_scale_two, g_gate_two], axis=-1)
    g_modul_b = g_modul.astype(jnp.bfloat16)
    gw_ada = grad_dot(saved['cond_act'], g_modul_b)
    gb_ada = lax.optimization_barrier(jnp.sum(g_modul, axis=0))
    cond_f = saved['cond_f']
    sigma = jax.nn.sigmoid(cond_f)
    g_cond = jnp.dot(g_modul_b, w_ada.T, preferred_element_type=jnp.float32) * (sigma * (1.0 + cond_f * (1.0 - sigma)))
    g_bias = jnp.concatenate([gb_ada, gb_query, gb_value, gb_out, gb_up, gb_down])
    grads = (gw_ada.reshape(-1), gw_qkv.reshape(-1), gw_out.reshape(-1), gw_up.reshape(-1), gw_down.reshape(-1), g_bias)
    return (g_inputs, g_cond, grads)

def reference(inputs, cond, cotan, counts, w_ada, w_qkv, w_out, w_up, w_down, biases):
    mats = (w_ada.reshape(D, 6 * D), w_qkv.reshape(D, 3 * D), w_out.reshape(D, D), w_up.reshape(D, FF), w_down.reshape(FF, D), biases)

    def grouped(array):
        return array.reshape((N_DEV, LAT_DEV) + array.shape[1:])

    def per_device(carry, slices):
        block_in, block_cond, block_cotan, block_count = slices
        live = (jnp.arange(LAT_DEV) < block_count).astype(jnp.float32)
        output, saved = device_forward(block_in, block_cond, live, mats)
        g_inputs, g_cond, grads = device_backward(block_cotan, live, mats, saved)
        summed = tuple((total + term for total, term in zip(carry, grads)))
        return (summed, (output, g_inputs, g_cond))
    initial = (jnp.zeros((6 * D * D,), jnp.float32), jnp.zeros((3 * D * D,), jnp.float32), jnp.zeros((D * D,), jnp.float32), jnp.zeros((D * FF,), jnp.float32), jnp.zeros((FF * D,), jnp.float32), jnp.zeros((10 * D + FF,), jnp.float32))
    totals, stacked = lax.scan(per_device, initial, (grouped(inputs), grouped(cond), grouped(cotan), counts))
    outputs, g_inputs, g_cond = stacked
    return (outputs.reshape(SLOTS, TOK, D), g_inputs.reshape(SLOTS, TOK, D), g_cond.reshape(SLOTS, D), totals[0], totals[1], totals[2], totals[3], totals[4], totals[5])
```

```python
import functools
import math

import jax
import jax.numpy as jnp
from jax import lax
from jax.experimental import pallas as pl
from jax.experimental.pallas import tpu as pltpu
from jax.sharding import PartitionSpec as P

D = 384
HEADS = 6
FF = 1536


EPS = 1e-06
GELU_C = 0.7978845608028654


def apply_gelu(pre):
    return 0.5 * pre * (1.0 + jnp.tanh(GELU_C * (pre + 0.044715 * pre * pre * pre)))


def gelu_slope(pre):
    tangent = jnp.tanh(GELU_C * (pre + 0.044715 * pre * pre * pre))
    return 0.5 * (1.0 + tangent) + 0.5 * pre * (1.0 - tangent * tangent) * GELU_C * (
        1.0 + 3.0 * 0.044715 * pre * pre
    )


def layer_norm(field):
    centred = field - jnp.mean(field, axis=-1, keepdims=True)
    inv_dev = lax.rsqrt(jnp.mean(centred * centred, axis=-1, keepdims=True) + EPS)
    return (centred * inv_dev, inv_dev)


def norm_backward(grad_h, normed, inv_dev):
    return inv_dev * (
        grad_h
        - jnp.mean(grad_h, axis=-1, keepdims=True)
        - normed * jnp.mean(grad_h * normed, axis=-1, keepdims=True)
    )


def flat_dot(left, right):
    result = jnp.dot(left.reshape(-1, left.shape[-1]), right, preferred_element_type=jnp.float32)
    return result.reshape(left.shape[:-1] + (right.shape[-1],))


def back_dot(left, right):
    result = lax.dot_general(
        left.reshape(-1, left.shape[-1]),
        right,
        (((1,), (1,)), ((), ())),
        preferred_element_type=jnp.float32,
    )
    return result.reshape(left.shape[:-1] + (right.shape[0],))


def grad_dot(left, right):
    return lax.dot_general(
        left.reshape(-1, left.shape[-1]),
        right.reshape(-1, right.shape[-1]),
        (((0,), (0,)), ((), ())),
        preferred_element_type=jnp.float32,
    )


def batched(form, left, right):
    return jnp.einsum(form, left, right, preferred_element_type=jnp.float32)


def split_bias(bias_all, width, hidden_units):
    bias_f = bias_all.astype(jnp.float32)
    return (
        bias_f[: 6 * width],
        bias_f[6 * width : 7 * width],
        bias_f[7 * width : 8 * width],
        bias_f[8 * width : 9 * width],
        bias_f[9 * width : 9 * width + hidden_units],
        bias_f[9 * width + hidden_units :],
    )


def shape_weights(gathered):
    flat_ada, flat_qkv, flat_out, flat_up, flat_down, bias_all = gathered
    return (
        flat_ada.reshape(D, 6 * D),
        flat_qkv.reshape(D, 3 * D),
        flat_out.reshape(D, D),
        flat_up.reshape(D, FF),
        flat_down.reshape(FF, D),
        bias_all,
    )


def device_forward(inputs, cond, live, mats):
    w_ada, w_qkv, w_out, w_up, w_down, bias_all = mats
    latents, tokens, width = inputs.shape
    hidden_units = w_up.shape[1]
    head_size = width // HEADS
    b_ada, b_query, b_value, b_out, b_up, b_down = split_bias(bias_all, width, hidden_units)
    cond_f = cond.astype(jnp.float32)
    cond_act = (cond_f * jax.nn.sigmoid(cond_f)).astype(jnp.bfloat16)
    modul = jnp.dot(cond_act, w_ada, preferred_element_type=jnp.float32) + b_ada
    pieces = [modul[:, None, index * width : (index + 1) * width] for index in range(6)]
    shift_one, scale_one, gate_one, shift_two, scale_two, gate_two = pieces
    resid = inputs.astype(jnp.float32)
    normed_one, inv_one = layer_norm(resid)
    mod_one = (normed_one * (1.0 + scale_one) + shift_one).astype(jnp.bfloat16)
    proj = flat_dot(mod_one, w_qkv)
    split_shape = (latents, tokens, HEADS, head_size)
    queries = (proj[..., :width] + b_query).astype(jnp.bfloat16).reshape(split_shape)
    keys_bf = proj[..., width : 2 * width].astype(jnp.bfloat16).reshape(split_shape)
    values_bf = (proj[..., 2 * width :] + b_value).astype(jnp.bfloat16).reshape(split_shape)
    factor = 1.0 / math.sqrt(head_size)
    scores = batched("lqhe,lkhe->lhqk", queries, keys_bf) * factor
    highest = jnp.max(scores, axis=-1, keepdims=True)
    expd = jnp.exp(scores - highest)
    totals = jnp.sum(expd, axis=-1, keepdims=True)
    probs = (expd / totals).astype(jnp.bfloat16)
    log_total = highest + jnp.log(totals)
    attended = (
        batched("lhqk,lkhe->lqhe", probs, values_bf)
        .astype(jnp.bfloat16)
        .reshape(latents, tokens, width)
    )
    att_out = flat_dot(attended, w_out) + b_out
    resid_one = resid + gate_one * att_out
    normed_two, inv_two = layer_norm(resid_one)
    mod_two = (normed_two * (1.0 + scale_two) + shift_two).astype(jnp.bfloat16)
    pre_act = flat_dot(mod_two, w_up) + b_up
    activ = apply_gelu(pre_act).astype(jnp.bfloat16)
    mlp_out = flat_dot(activ, w_down) + b_down
    output = (resid_one + gate_two * mlp_out) * live[:, None, None]
    saved = dict(
        cond_f=cond_f,
        cond_act=cond_act,
        scale_one=scale_one,
        gate_one=gate_one,
        scale_two=scale_two,
        gate_two=gate_two,
        normed_one=normed_one,
        inv_one=inv_one,
        mod_one=mod_one,
        queries=queries,
        keys_bf=keys_bf,
        values_bf=values_bf,
        log_total=log_total,
        attended=attended,
        att_out=att_out,
        normed_two=normed_two,
        inv_two=inv_two,
        mod_two=mod_two,
        pre_act=pre_act,
        activ=activ,
        mlp_out=mlp_out,
    )
    return (output, saved)


def device_backward(cotan, live, mats, saved):
    w_ada, w_qkv, w_out, w_up, w_down, bias_all = mats
    latents, tokens, width = cotan.shape
    head_size = width // HEADS
    factor = 1.0 / math.sqrt(head_size)
    grad_y = cotan.astype(jnp.float32) * live[:, None, None]
    g_gate_two = jnp.sum(grad_y * saved["mlp_out"], axis=1)
    g_mlp = grad_y * saved["gate_two"]
    g_mlp_b = g_mlp.astype(jnp.bfloat16)
    gw_down = grad_dot(saved["activ"], g_mlp_b)
    gb_down = jnp.sum(g_mlp, axis=(0, 1))
    g_pre = back_dot(g_mlp_b, w_down) * gelu_slope(saved["pre_act"])
    g_pre_b = g_pre.astype(jnp.bfloat16)
    gw_up = grad_dot(saved["mod_two"], g_pre_b)
    gb_up = jnp.sum(g_pre, axis=(0, 1))
    g_mod_two = back_dot(g_pre_b, w_up)
    g_scale_two = jnp.sum(g_mod_two * saved["normed_two"], axis=1)
    g_shift_two = jnp.sum(g_mod_two, axis=1)
    g_resid_one = grad_y + norm_backward(
        g_mod_two * (1.0 + saved["scale_two"]), saved["normed_two"], saved["inv_two"]
    )
    g_gate_one = jnp.sum(g_resid_one * saved["att_out"], axis=1)
    g_attn = g_resid_one * saved["gate_one"]
    g_attn_b = g_attn.astype(jnp.bfloat16)
    gw_out = grad_dot(saved["attended"], g_attn_b)
    gb_out = jnp.sum(g_attn, axis=(0, 1))
    split_shape = (latents, tokens, HEADS, head_size)
    g_attended = back_dot(g_attn_b, w_out).astype(jnp.bfloat16).reshape(split_shape)
    queries, keys_bf, values_bf = (saved["queries"], saved["keys_bf"], saved["values_bf"])
    scores = batched("lqhe,lkhe->lhqk", queries, keys_bf) * factor
    probs_f = jnp.exp(scores - saved["log_total"])
    probs_b = probs_f.astype(jnp.bfloat16)
    g_values = batched("lhqk,lqhe->lkhe", probs_b, g_attended)
    g_probs = batched("lqhe,lkhe->lhqk", g_attended, values_bf)
    row_dot = jnp.sum(
        g_attended.astype(jnp.float32) * saved["attended"].astype(jnp.float32).reshape(split_shape),
        axis=-1,
    )
    row_dot = jnp.transpose(row_dot, (0, 2, 1))[..., None]
    g_scores = (probs_f * (g_probs - row_dot) * factor).astype(jnp.bfloat16)
    g_query = batched("lhqk,lkhe->lqhe", g_scores, keys_bf).reshape(latents, tokens, width)
    g_key = batched("lhqk,lqhe->lkhe", g_scores, queries).reshape(latents, tokens, width)
    g_values = g_values.reshape(latents, tokens, width)
    g_proj_b = jnp.concatenate([g_query, g_key, g_values], axis=-1).astype(jnp.bfloat16)
    gw_qkv = grad_dot(saved["mod_one"], g_proj_b)
    gb_query = jnp.sum(g_query, axis=(0, 1))
    gb_value = jnp.sum(g_values, axis=(0, 1))
    g_mod_one = back_dot(g_proj_b, w_qkv)
    g_scale_one = jnp.sum(g_mod_one * saved["normed_one"], axis=1)
    g_shift_one = jnp.sum(g_mod_one, axis=1)
    g_inputs = g_resid_one + norm_backward(
        g_mod_one * (1.0 + saved["scale_one"]), saved["normed_one"], saved["inv_one"]
    )
    g_modul = jnp.concatenate(
        [g_shift_one, g_scale_one, g_gate_one, g_shift_two, g_scale_two, g_gate_two], axis=-1
    )
    g_modul_b = g_modul.astype(jnp.bfloat16)
    gw_ada = grad_dot(saved["cond_act"], g_modul_b)
    gb_ada = jnp.sum(g_modul, axis=0)
    cond_f = saved["cond_f"]
    sigma = jax.nn.sigmoid(cond_f)
    g_cond = back_dot(g_modul_b, w_ada) * (sigma * (1.0 + cond_f * (1.0 - sigma)))
    g_bias = jnp.concatenate([gb_ada, gb_query, gb_value, gb_out, gb_up, gb_down])
    grads = (
        gw_ada.reshape(-1),
        gw_qkv.reshape(-1),
        gw_out.reshape(-1),
        gw_up.reshape(-1),
        gw_down.reshape(-1),
        g_bias,
    )
    return (g_inputs, g_cond, grads)


LANE = 128
ROWS = 656
HALF = 336
GRID = (4, 2, 2, 2)
LINE = [(0, 0)] + [(side, step) for step in (1, 2, 3) for side in (-1, 1)]


def spot():
    me = lax.axis_index("dev")
    return me // 8, (me // 4) % 2, (me // 2) % 2, me % 2


def number(z, y, x, c):
    return ((z * 2 + y) * 2 + x) * 2 + c


def greet(z, y, x, c):
    barrier = pltpu.get_barrier_semaphore()
    for other in (
        number(z, y, x, 1 - c),
        number(z, y, 1 - x, c),
        number(z, 1 - y, x, c),
        number((z + 1) % 4, y, x, c),
        number((z + 3) % 4, y, x, c),
    ):
        pl.semaphore_signal(
            barrier, inc=1, device_id=(other,), device_id_type=pl.DeviceIdType.MESH
        )
    pl.semaphore_wait(barrier, 5)


def remote(src, dst, send, recv, device):
    return pltpu.make_async_remote_copy(
        src_ref=src,
        dst_ref=dst,
        send_sem=send,
        recv_sem=recv,
        device_id=(device,),
        device_id_type=pl.DeviceIdType.MESH,
    )


def gather_kernel(own_ref, all_ref, own_sem, line_s, line_r, side_s, side_r, core_s, core_r):
    z, y, x, c = spot()
    mine = pltpu.make_async_copy(own_ref, all_ref.at[number(z, y, x, c)], own_sem)
    mine.start()
    greet(z, y, x, c)
    mine.wait()
    top = pl.ds(0, HALF)
    low = pl.ds(HALF, ROWS - HALF)
    to_x, to_y, to_core = number(z, y, 1 - x, c), number(z, 1 - y, x, c), number(z, y, x, 1 - c)

    def level(j):
        return z + LINE[j][0] * LINE[j][1]

    def present(j):
        return jnp.logical_and(level(j) >= 0, level(j) <= 3)

    def same(ref, send, recv, device):
        return remote(ref, ref, send, recv, device)

    def line_copy(j, way):
        side, step = LINE[j]
        later = LINE.index((-way, step + 1))
        slot = all_ref.at[number(level(j), y, x, c)]
        return same(slot, line_s.at[later], line_r.at[later], number(z + way, y, x, c))

    def line_ways(j):
        side, step = LINE[j]
        if step == 3:
            return ()
        return (1, -1) if step == 0 else (-side,)

    def way_open(way):
        return z < 3 if way == 1 else z > 0

    def side_copy(j, which):
        zo = level(j)
        if which == 0:
            return same(all_ref.at[number(zo, y, x, c)], side_s.at[j, 0], side_r.at[j, 0], to_y)
        if which == 1:
            return same(all_ref.at[number(zo, y, x, c)], side_s.at[j, 1], side_r.at[j, 1], to_x)
        if which == 2:
            return same(
                all_ref.at[number(zo, 1 - y, x, c), top], side_s.at[j, 2], side_r.at[j, 2], to_x
            )
        return same(
            all_ref.at[number(zo, y, 1 - x, c), low], side_s.at[j, 3], side_r.at[j, 3], to_y
        )

    def core_copy(j, which):
        yy, xx = ((y, x), (1 - y, x), (y, 1 - x), (1 - y, 1 - x))[which]
        slot = all_ref.at[number(level(j), yy, xx, c)]
        return same(slot, core_s.at[j, which], core_r.at[j, which], to_core)

    def first(j):
        @pl.when(present(j))
        def _():
            side, step = LINE[j]
            if step:
                before = LINE.index((side, step - 1)) if step > 1 else 0
                slot = all_ref.at[number(level(j), y, x, c)]
                same(slot, line_s.at[j], line_r.at[j], number(z + side, y, x, c)).wait_recv()
            for way in line_ways(j):

                @pl.when(way_open(way))
                def _(way=way):
                    line_copy(j, way).start()

            side_copy(j, 0).start()
            side_copy(j, 1).start()
            core_copy(j, 0).start()

    def second(j):
        @pl.when(present(j))
        def _():
            side_copy(j, 0).wait_recv()
            side_copy(j, 2).start()
            core_copy(j, 1).start()
            side_copy(j, 1).wait_recv()
            side_copy(j, 3).start()
            core_copy(j, 2).start()

    def third(j):
        @pl.when(present(j))
        def _():
            side_copy(j, 2).wait_recv()
            side_copy(j, 3).wait_recv()
            core_copy(j, 3).start()

    count = len(LINE)
    for t in range(count + 4):
        if t < count:
            first(t)
        if 0 <= t - 2 < count:
            second(t - 2)
        if 0 <= t - 4 < count:
            third(t - 4)
    for j in range(count):

        @pl.when(present(j))
        def _(j=j):
            for which in range(4):
                core_copy(j, which).wait_recv()
                core_copy(j, which).wait_send()
                side_copy(j, which).wait_send()
            for way in line_ways(j):

                @pl.when(way_open(way))
                def _(way=way):
                    line_copy(j, way).wait_send()


def gather_all(own):
    sems = pltpu.SemaphoreType.DMA
    count = len(LINE)
    return pl.pallas_call(
        gather_kernel,
        out_shape=jax.ShapeDtypeStruct((32, ROWS, LANE), own.dtype),
        in_specs=[pl.BlockSpec(memory_space=pltpu.VMEM)],
        out_specs=pl.BlockSpec(memory_space=pltpu.VMEM),
        scratch_shapes=[
            sems(()),
            sems((count,)),
            sems((count,)),
            sems((count, 4)),
            sems((count, 4)),
            sems((count, 4)),
            sems((count, 4)),
        ],
        compiler_params=pltpu.CompilerParams(collective_id=1, has_side_effects=True),
        name="gather_shares",
    )(own)


def scatter_kernel(
    g_ref, out_ref, acc, core_b, diag_b, y_b, x_b, line_b,
    core_s, core_r, diag_s, diag_r, side_s, side_r, line_s, line_r,
):
    z, y, x, c = spot()
    greet(z, y, x, c)
    top = pl.ds(0, HALF)
    low = pl.ds(HALF, ROWS - HALF)
    to_x, to_y, to_core = number(z, y, 1 - x, c), number(z, 1 - y, x, c), number(z, y, x, 1 - c)
    order = LINE[::-1]
    count = len(order)

    def level(j):
        return z + order[j][0] * order[j][1]

    def present(j):
        return jnp.logical_and(level(j) >= 0, level(j) <= 3)

    def spots(which):
        return ((y, x), (1 - y, x), (y, 1 - x), (1 - y, 1 - x))[which]

    def own_term(j, which):
        yy, xx = spots(which)
        return g_ref[number(level(j), yy, xx, c)].astype(jnp.float32)

    def core_copy(j, which):
        yy, xx = spots(which)
        return remote(
            g_ref.at[number(level(j), yy, xx, 1 - c)],
            core_b.at[j, which],
            core_s.at[j, which],
            core_r.at[j, which],
            to_core,
        )

    def diag_copy(j, which):
        part = (top, low)[which]
        return remote(
            acc.at[j, 3, part],
            diag_b.at[j, part],
            diag_s.at[j, which],
            diag_r.at[j, which],
            (to_x, to_y)[which],
        )

    def side_copy(j, which):
        return remote(
            acc.at[j, 1 + which],
            (y_b, x_b)[which].at[j],
            side_s.at[j, which],
            side_r.at[j, which],
            (to_y, to_x)[which],
        )

    def line_slot(side, step):
        return step if side == 1 else 3 + step

    def line_copy(j):
        side, step = order[j]
        slot = line_slot(side, step - 1)
        return remote(
            acc.at[j, 0],
            line_b.at[slot],
            line_s.at[j],
            line_r.at[slot],
            number(z + side, y, x, c),
        )

    def line_take(side, step):
        slot = line_slot(side, step)
        remote(
            acc.at[0, 0], line_b.at[slot], line_s.at[0], line_r.at[slot], number(z - side, y, x, c)
        ).wait_recv()
        out_ref[...] += line_b[slot].astype(jnp.float32)

    for which in (3, 1, 2, 0):
        for j in range(count):

            @pl.when(present(j))
            def _(j=j, which=which):
                core_copy(j, which).start()

    def first(j):
        @pl.when(present(j))
        def _():
            core_copy(j, 3).wait_recv()
            total = own_term(j, 3) + core_b[j, 3].astype(jnp.float32)
            acc[j, 3] = total.astype(jnp.bfloat16)
            diag_copy(j, 0).start()
            diag_copy(j, 1).start()

    def second(j):
        @pl.when(present(j))
        def _():
            core_copy(j, 1).wait_recv()
            diag_copy(j, 0).wait_recv()
            total = own_term(j, 1) + core_b[j, 1].astype(jnp.float32)
            acc[j, 1, top] = (total[:HALF] + diag_b[j, top].astype(jnp.float32)).astype(jnp.bfloat16)
            acc[j, 1, low] = total[HALF:].astype(jnp.bfloat16)
            side_copy(j, 0).start()
            core_copy(j, 2).wait_recv()
            diag_copy(j, 1).wait_recv()
            total = own_term(j, 2) + core_b[j, 2].astype(jnp.float32)
            acc[j, 2, top] = total[:HALF].astype(jnp.bfloat16)
            acc[j, 2, low] = (total[HALF:] + diag_b[j, low].astype(jnp.float32)).astype(jnp.bfloat16)
            side_copy(j, 1).start()

    def third(j):
        side, step = order[j]

        @pl.when(present(j))
        def _():
            core_copy(j, 0).wait_recv()
            side_copy(j, 0).wait_recv()
            side_copy(j, 1).wait_recv()
            out_ref[...] = (
                own_term(j, 0)
                + core_b[j, 0].astype(jnp.float32)
                + y_b[j].astype(jnp.float32)
                + x_b[j].astype(jnp.float32)
            )
            if side >= 0:

                @pl.when(z > 0)
                def _():
                    line_take(1, step)

            if side <= 0:

                @pl.when(z < 3)
                def _():
                    line_take(-1, step)

            if step:
                acc[j, 0] = out_ref[...].astype(jnp.bfloat16)
                line_copy(j).start()

    for t in range(count + 4):
        if t < count:
            first(t)
        if 0 <= t - 2 < count:
            second(t - 2)
        if 0 <= t - 4 < count:
            third(t - 4)
    for j in range(count):

        @pl.when(present(j))
        def _(j=j):
            for which in range(4):
                core_copy(j, which).wait_send()
            for which in range(2):
                diag_copy(j, which).wait_send()
                side_copy(j, which).wait_send()
            if order[j][1]:
                line_copy(j).wait_send()


def scatter_sum(parts):
    sems = pltpu.SemaphoreType.DMA
    count = len(LINE)
    share = (ROWS, LANE)
    return pl.pallas_call(
        scatter_kernel,
        out_shape=jax.ShapeDtypeStruct(share, jnp.float32),
        in_specs=[pl.BlockSpec(memory_space=pltpu.VMEM)],
        out_specs=pl.BlockSpec(memory_space=pltpu.VMEM),
        scratch_shapes=[
            pltpu.VMEM((count, 4) + share, jnp.bfloat16),
            pltpu.VMEM((count, 4) + share, jnp.bfloat16),
            pltpu.VMEM((count,) + share, jnp.bfloat16),
            pltpu.VMEM((count,) + share, jnp.bfloat16),
            pltpu.VMEM((count,) + share, jnp.bfloat16),
            pltpu.VMEM((6,) + share, jnp.bfloat16),
            sems((count, 4)),
            sems((count, 4)),
            sems((count, 2)),
            sems((count, 2)),
            sems((count, 2)),
            sems((count, 2)),
            sems((count,)),
            sems((6,)),
        ],
        compiler_params=pltpu.CompilerParams(collective_id=2, has_side_effects=True),
        name="scatter_gradients",
    )(parts)


SIZES = (6 * D * D, 3 * D * D, D * D, D * FF, FF * D, 10 * D + FF)


def packed(pieces, lead, dtype):
    flat = jnp.concatenate([p.astype(dtype).reshape(lead + (-1,)) for p in pieces], axis=-1)
    pad = ROWS * LANE - flat.shape[-1]
    flat = jnp.concatenate([flat, jnp.zeros(lead + (pad,), dtype)], axis=-1)
    return flat.reshape(lead + (ROWS, LANE))


def unpacked(block, devices):
    flat = block.reshape(block.shape[:-2] + (-1,))
    start = 0
    pieces = []
    for size in SIZES:
        width = size // devices
        pieces.append(flat[..., start : start + width].reshape(-1))
        start += width
    return pieces


def shards(devices, inputs, cond, cotan, counts, *weights):
    latents = inputs.shape[0]
    live = (jnp.arange(latents) < counts[0]).astype(jnp.float32)
    small = devices == 32
    if small:
        gathered = unpacked(gather_all(packed(weights, (), jnp.bfloat16)), devices)
    else:
        gathered = [lax.all_gather(w, "dev", axis=0, tiled=True) for w in weights]
    mats = shape_weights(gathered)
    output, saved = device_forward(inputs, cond, live, mats)
    g_inputs, g_cond, grads = device_backward(cotan, live, mats, saved)
    if small:
        parts = packed([g.reshape(devices, -1) for g in grads], (devices,), jnp.bfloat16)
        shares = unpacked(scatter_sum(parts), devices)
    else:
        shares = [
            lax.psum_scatter(g, "dev", scatter_dimension=0, tiled=True) for g in grads
        ]
    return (output, g_inputs, g_cond, *shares)


def solution(mesh):
    in_specs = (
        P("dev", None, None),
        P("dev", None),
        P("dev", None, None),
        P("dev"),
        P("dev"),
        P("dev"),
        P("dev"),
        P("dev"),
        P("dev"),
        P("dev"),
    )
    out_specs = (
        P("dev", None, None),
        P("dev", None, None),
        P("dev", None),
        P("dev"),
        P("dev"),
        P("dev"),
        P("dev"),
        P("dev"),
        P("dev"),
    )
    return jax.shard_map(functools.partial(shards, mesh.shape["dev"]), mesh=mesh, in_specs=in_specs, out_specs=out_specs, check_vma=False)
```

```python
import functools
import math

import jax
import jax.numpy as jnp
from jax import lax
from jax.experimental import pallas as pl
from jax.experimental.pallas import tpu as pltpu
from jax.sharding import PartitionSpec as P

D = 384
HEADS = 6
FF = 1536


EPS = 1e-06
GELU_C = 0.7978845608028654


def apply_gelu(pre):
    return 0.5 * pre * (1.0 + jnp.tanh(GELU_C * (pre + 0.044715 * pre * pre * pre)))


def gelu_slope(pre):
    tangent = jnp.tanh(GELU_C * (pre + 0.044715 * pre * pre * pre))
    return 0.5 * (1.0 + tangent) + 0.5 * pre * (1.0 - tangent * tangent) * GELU_C * (
        1.0 + 3.0 * 0.044715 * pre * pre
    )


def layer_norm(field):
    centred = field - jnp.mean(field, axis=-1, keepdims=True)
    inv_dev = lax.rsqrt(jnp.mean(centred * centred, axis=-1, keepdims=True) + EPS)
    return (centred * inv_dev, inv_dev)


def norm_backward(grad_h, normed, inv_dev):
    return inv_dev * (
        grad_h
        - jnp.mean(grad_h, axis=-1, keepdims=True)
        - normed * jnp.mean(grad_h * normed, axis=-1, keepdims=True)
    )


def flat_dot(left, right):
    result = jnp.dot(left.reshape(-1, left.shape[-1]), right, preferred_element_type=jnp.float32)
    return result.reshape(left.shape[:-1] + (right.shape[-1],))


def back_dot(left, right):
    result = lax.dot_general(
        left.reshape(-1, left.shape[-1]),
        right,
        (((1,), (1,)), ((), ())),
        preferred_element_type=jnp.float32,
    )
    return result.reshape(left.shape[:-1] + (right.shape[0],))


def grad_dot(left, right):
    return lax.dot_general(
        left.reshape(-1, left.shape[-1]),
        right.reshape(-1, right.shape[-1]),
        (((0,), (0,)), ((), ())),
        preferred_element_type=jnp.float32,
    )


def batched(form, left, right):
    return jnp.einsum(form, left, right, preferred_element_type=jnp.float32)


def split_bias(bias_all, width, hidden_units):
    bias_f = bias_all.astype(jnp.float32)
    return (
        bias_f[: 6 * width],
        bias_f[6 * width : 7 * width],
        bias_f[7 * width : 8 * width],
        bias_f[8 * width : 9 * width],
        bias_f[9 * width : 9 * width + hidden_units],
        bias_f[9 * width + hidden_units :],
    )


def shape_weights(gathered):
    flat_ada, flat_qkv, flat_out, flat_up, flat_down, bias_all = gathered
    return (
        flat_ada.reshape(D, 6 * D),
        flat_qkv.reshape(D, 3 * D),
        flat_out.reshape(D, D),
        flat_up.reshape(D, FF),
        flat_down.reshape(FF, D),
        bias_all,
    )


def device_forward(inputs, cond, live, mats):
    w_ada, w_qkv, w_out, w_up, w_down, bias_all = mats
    latents, tokens, width = inputs.shape
    hidden_units = w_up.shape[1]
    head_size = width // HEADS
    b_ada, b_query, b_value, b_out, b_up, b_down = split_bias(bias_all, width, hidden_units)
    cond_f = cond.astype(jnp.float32)
    cond_act = (cond_f * jax.nn.sigmoid(cond_f)).astype(jnp.bfloat16)
    modul = jnp.dot(cond_act, w_ada, preferred_element_type=jnp.float32) + b_ada
    pieces = [modul[:, None, index * width : (index + 1) * width] for index in range(6)]
    shift_one, scale_one, gate_one, shift_two, scale_two, gate_two = pieces
    resid = inputs.astype(jnp.float32)
    normed_one, inv_one = layer_norm(resid)
    mod_one = (normed_one * (1.0 + scale_one) + shift_one).astype(jnp.bfloat16)
    proj = flat_dot(mod_one, w_qkv)
    split_shape = (latents, tokens, HEADS, head_size)
    queries = (proj[..., :width] + b_query).astype(jnp.bfloat16).reshape(split_shape)
    keys_bf = proj[..., width : 2 * width].astype(jnp.bfloat16).reshape(split_shape)
    values_bf = (proj[..., 2 * width :] + b_value).astype(jnp.bfloat16).reshape(split_shape)
    factor = 1.0 / math.sqrt(head_size)
    scores = batched("lqhe,lkhe->lhqk", queries, keys_bf) * factor
    highest = jnp.max(scores, axis=-1, keepdims=True)
    expd = jnp.exp(scores - highest)
    totals = jnp.sum(expd, axis=-1, keepdims=True)
    probs = (expd / totals).astype(jnp.bfloat16)
    log_total = highest + jnp.log(totals)
    attended = (
        batched("lhqk,lkhe->lqhe", probs, values_bf)
        .astype(jnp.bfloat16)
        .reshape(latents, tokens, width)
    )
    att_out = flat_dot(attended, w_out) + b_out
    resid_one = resid + gate_one * att_out
    normed_two, inv_two = layer_norm(resid_one)
    mod_two = (normed_two * (1.0 + scale_two) + shift_two).astype(jnp.bfloat16)
    pre_act = flat_dot(mod_two, w_up) + b_up
    activ = apply_gelu(pre_act).astype(jnp.bfloat16)
    mlp_out = flat_dot(activ, w_down) + b_down
    output = (resid_one + gate_two * mlp_out) * live[:, None, None]
    saved = dict(
        cond_f=cond_f,
        cond_act=cond_act,
        scale_one=scale_one,
        gate_one=gate_one,
        scale_two=scale_two,
        gate_two=gate_two,
        normed_one=normed_one,
        inv_one=inv_one,
        mod_one=mod_one,
        queries=queries,
        keys_bf=keys_bf,
        values_bf=values_bf,
        log_total=log_total,
        attended=attended,
        att_out=att_out,
        normed_two=normed_two,
        inv_two=inv_two,
        mod_two=mod_two,
        pre_act=pre_act,
        activ=activ,
        mlp_out=mlp_out,
    )
    return (output, saved)


def device_backward(cotan, live, mats, saved):
    w_ada, w_qkv, w_out, w_up, w_down, bias_all = mats
    latents, tokens, width = cotan.shape
    head_size = width // HEADS
    factor = 1.0 / math.sqrt(head_size)
    grad_y = cotan.astype(jnp.float32) * live[:, None, None]
    g_gate_two = jnp.sum(grad_y * saved["mlp_out"], axis=1)
    g_mlp = grad_y * saved["gate_two"]
    g_mlp_b = g_mlp.astype(jnp.bfloat16)
    gw_down = grad_dot(saved["activ"], g_mlp_b)
    gb_down = jnp.sum(g_mlp, axis=(0, 1))
    g_pre = back_dot(g_mlp_b, w_down) * gelu_slope(saved["pre_act"])
    g_pre_b = g_pre.astype(jnp.bfloat16)
    gw_up = grad_dot(saved["mod_two"], g_pre_b)
    gb_up = jnp.sum(g_pre, axis=(0, 1))
    g_mod_two = back_dot(g_pre_b, w_up)
    g_scale_two = jnp.sum(g_mod_two * saved["normed_two"], axis=1)
    g_shift_two = jnp.sum(g_mod_two, axis=1)
    g_resid_one = grad_y + norm_backward(
        g_mod_two * (1.0 + saved["scale_two"]), saved["normed_two"], saved["inv_two"]
    )
    g_gate_one = jnp.sum(g_resid_one * saved["att_out"], axis=1)
    g_attn = g_resid_one * saved["gate_one"]
    g_attn_b = g_attn.astype(jnp.bfloat16)
    gw_out = grad_dot(saved["attended"], g_attn_b)
    gb_out = jnp.sum(g_attn, axis=(0, 1))
    split_shape = (latents, tokens, HEADS, head_size)
    g_attended = back_dot(g_attn_b, w_out).astype(jnp.bfloat16).reshape(split_shape)
    queries, keys_bf, values_bf = (saved["queries"], saved["keys_bf"], saved["values_bf"])
    scores = batched("lqhe,lkhe->lhqk", queries, keys_bf) * factor
    probs_f = jnp.exp(scores - saved["log_total"])
    probs_b = probs_f.astype(jnp.bfloat16)
    g_values = batched("lhqk,lqhe->lkhe", probs_b, g_attended)
    g_probs = batched("lqhe,lkhe->lhqk", g_attended, values_bf)
    row_dot = jnp.sum(
        g_attended.astype(jnp.float32) * saved["attended"].astype(jnp.float32).reshape(split_shape),
        axis=-1,
    )
    row_dot = jnp.transpose(row_dot, (0, 2, 1))[..., None]
    g_scores = (probs_f * (g_probs - row_dot) * factor).astype(jnp.bfloat16)
    g_query = batched("lhqk,lkhe->lqhe", g_scores, keys_bf).reshape(latents, tokens, width)
    g_key = batched("lhqk,lqhe->lkhe", g_scores, queries).reshape(latents, tokens, width)
    g_values = g_values.reshape(latents, tokens, width)
    g_proj_b = jnp.concatenate([g_query, g_key, g_values], axis=-1).astype(jnp.bfloat16)
    gw_qkv = grad_dot(saved["mod_one"], g_proj_b)
    gb_query = jnp.sum(g_query, axis=(0, 1))
    gb_value = jnp.sum(g_values, axis=(0, 1))
    g_mod_one = back_dot(g_proj_b, w_qkv)
    g_scale_one = jnp.sum(g_mod_one * saved["normed_one"], axis=1)
    g_shift_one = jnp.sum(g_mod_one, axis=1)
    g_inputs = g_resid_one + norm_backward(
        g_mod_one * (1.0 + saved["scale_one"]), saved["normed_one"], saved["inv_one"]
    )
    g_modul = jnp.concatenate(
        [g_shift_one, g_scale_one, g_gate_one, g_shift_two, g_scale_two, g_gate_two], axis=-1
    )
    g_modul_b = g_modul.astype(jnp.bfloat16)
    gw_ada = grad_dot(saved["cond_act"], g_modul_b)
    gb_ada = jnp.sum(g_modul, axis=0)
    cond_f = saved["cond_f"]
    sigma = jax.nn.sigmoid(cond_f)
    g_cond = back_dot(g_modul_b, w_ada) * (sigma * (1.0 + cond_f * (1.0 - sigma)))
    g_bias = jnp.concatenate([gb_ada, gb_query, gb_value, gb_out, gb_up, gb_down])
    grads = (
        gw_ada.reshape(-1),
        gw_qkv.reshape(-1),
        gw_out.reshape(-1),
        gw_up.reshape(-1),
        gw_down.reshape(-1),
        g_bias,
    )
    return (g_inputs, g_cond, grads)


LANE = 128
ROWS = 672
SLOT = 56
COUNTS_PER_ROW = (18, 9, 3, 12, 12)
HALF = 336
GRID = (4, 2, 2, 2)
LINE = [(0, 0)] + [(side, step) for step in (1, 2, 3) for side in (-1, 1)]


def spot():
    me = lax.axis_index("dev")
    return me // 8, (me // 4) % 2, (me // 2) % 2, me % 2


def number(z, y, x, c):
    return ((z * 2 + y) * 2 + x) * 2 + c


def greet(z, y, x, c):
    barrier = pltpu.get_barrier_semaphore()
    for other in (
        number(z, y, x, 1 - c),
        number(z, y, 1 - x, c),
        number(z, 1 - y, x, c),
        number((z + 1) % 4, y, x, c),
        number((z + 3) % 4, y, x, c),
    ):
        pl.semaphore_signal(
            barrier, inc=1, device_id=(other,), device_id_type=pl.DeviceIdType.MESH
        )
    pl.semaphore_wait(barrier, 5)


def remote(src, dst, send, recv, device):
    return pltpu.make_async_remote_copy(
        src_ref=src,
        dst_ref=dst,
        send_sem=send,
        recv_sem=recv,
        device_id=(device,),
        device_id_type=pl.DeviceIdType.MESH,
    )


def gather_kernel(
    ada_ref, qkv_ref, out_ref, up_ref, down_ref, bias_ref, all_ref,
    loose, laid, own, own_sem, line_s, line_r, side_s, side_r, core_s, core_r,
):
    z, y, x, c = spot()
    laid[...] = jnp.zeros_like(laid)
    base = start = 0
    for ref, count in zip((ada_ref, qkv_ref, out_ref, up_ref, down_ref), COUNTS_PER_ROW):
        loose[base : base + 12 * count, :] = ref[...].astype(jnp.float32)
        for i in range(12):
            laid[i * SLOT + start : i * SLOT + start + count, :] = loose[
                base + i * count : base + (i + 1) * count, :
            ]
        base += 12 * count
        start += count
    laid[start : start + 2, :] = bias_ref[...].astype(jnp.float32)
    own[...] = laid[...].astype(jnp.bfloat16)
    mine = pltpu.make_async_copy(own, all_ref.at[number(z, y, x, c)], own_sem)
    mine.start()
    greet(z, y, x, c)
    mine.wait()
    top = pl.ds(0, HALF)
    low = pl.ds(HALF, ROWS - HALF)
    to_x, to_y, to_core = number(z, y, 1 - x, c), number(z, 1 - y, x, c), number(z, y, x, 1 - c)

    def level(j):
        return z + LINE[j][0] * LINE[j][1]

    def present(j):
        return jnp.logical_and(level(j) >= 0, level(j) <= 3)

    def same(ref, send, recv, device):
        return remote(ref, ref, send, recv, device)

    def line_copy(j, way):
        side, step = LINE[j]
        later = LINE.index((-way, step + 1))
        slot = all_ref.at[number(level(j), y, x, c)]
        return same(slot, line_s.at[later], line_r.at[later], number(z + way, y, x, c))

    def line_ways(j):
        side, step = LINE[j]
        if step == 3:
            return ()
        return (1, -1) if step == 0 else (-side,)

    def way_open(way):
        return z < 3 if way == 1 else z > 0

    def side_copy(j, which):
        zo = level(j)
        if which == 0:
            return same(all_ref.at[number(zo, y, x, c)], side_s.at[j, 0], side_r.at[j, 0], to_y)
        if which == 1:
            return same(all_ref.at[number(zo, y, x, c)], side_s.at[j, 1], side_r.at[j, 1], to_x)
        if which == 2:
            return same(
                all_ref.at[number(zo, 1 - y, x, c), top], side_s.at[j, 2], side_r.at[j, 2], to_x
            )
        return same(
            all_ref.at[number(zo, y, 1 - x, c), low], side_s.at[j, 3], side_r.at[j, 3], to_y
        )

    def core_copy(j, which):
        yy, xx = ((y, x), (1 - y, x), (y, 1 - x), (1 - y, 1 - x))[which]
        slot = all_ref.at[number(level(j), yy, xx, c)]
        return same(slot, core_s.at[j, which], core_r.at[j, which], to_core)

    def first(j):
        @pl.when(present(j))
        def _():
            side, step = LINE[j]
            if step:
                before = LINE.index((side, step - 1)) if step > 1 else 0
                slot = all_ref.at[number(level(j), y, x, c)]
                same(slot, line_s.at[j], line_r.at[j], number(z + side, y, x, c)).wait_recv()
            for way in line_ways(j):

                @pl.when(way_open(way))
                def _(way=way):
                    line_copy(j, way).start()

            side_copy(j, 0).start()
            side_copy(j, 1).start()
            core_copy(j, 0).start()

    def second(j):
        @pl.when(present(j))
        def _():
            side_copy(j, 0).wait_recv()
            side_copy(j, 2).start()
            core_copy(j, 1).start()
            side_copy(j, 1).wait_recv()
            side_copy(j, 3).start()
            core_copy(j, 2).start()

    def third(j):
        @pl.when(present(j))
        def _():
            side_copy(j, 2).wait_recv()
            side_copy(j, 3).wait_recv()
            core_copy(j, 3).start()

    count = len(LINE)
    for t in range(count + 4):
        if t < count:
            first(t)
        if 0 <= t - 2 < count:
            second(t - 2)
        if 0 <= t - 4 < count:
            third(t - 4)
    for j in range(count):

        @pl.when(present(j))
        def _(j=j):
            for which in range(4):
                core_copy(j, which).wait_recv()
                core_copy(j, which).wait_send()
                side_copy(j, which).wait_send()
            for way in line_ways(j):

                @pl.when(way_open(way))
                def _(way=way):
                    line_copy(j, way).wait_send()


def gather_all(*pieces):
    sems = pltpu.SemaphoreType.DMA
    count = len(LINE)
    return pl.pallas_call(
        gather_kernel,
        out_shape=jax.ShapeDtypeStruct((32, ROWS, LANE), jnp.bfloat16),
        in_specs=[pl.BlockSpec(memory_space=pltpu.VMEM)] * 6,
        out_specs=pl.BlockSpec(memory_space=pltpu.VMEM),
        scratch_shapes=[
            pltpu.VMEM((12 * sum(COUNTS_PER_ROW), LANE), jnp.float32),
            pltpu.VMEM((ROWS, LANE), jnp.float32),
            pltpu.VMEM((ROWS, LANE), jnp.bfloat16),
            sems(()),
            sems((count,)),
            sems((count,)),
            sems((count, 4)),
            sems((count, 4)),
            sems((count, 4)),
            sems((count, 4)),
        ],
        compiler_params=pltpu.CompilerParams(collective_id=1, has_side_effects=True),
        name="gather_shares",
    )(*pieces)


def scatter_kernel(
    g_ref, ada_ref, qkv_ref, wo_ref, up_ref, down_ref, bias_ref,
    out_ref, acc, core_b, diag_b, y_b, x_b, line_b,
    core_s, core_r, diag_s, diag_r, side_s, side_r, line_s, line_r,
):
    z, y, x, c = spot()
    greet(z, y, x, c)
    top = pl.ds(0, HALF)
    low = pl.ds(HALF, ROWS - HALF)
    to_x, to_y, to_core = number(z, y, 1 - x, c), number(z, 1 - y, x, c), number(z, y, x, 1 - c)
    order = LINE[::-1]
    count = len(order)

    def level(j):
        return z + order[j][0] * order[j][1]

    def present(j):
        return jnp.logical_and(level(j) >= 0, level(j) <= 3)

    def spots(which):
        return ((y, x), (1 - y, x), (y, 1 - x), (1 - y, 1 - x))[which]

    def own_term(j, which):
        yy, xx = spots(which)
        return g_ref[number(level(j), yy, xx, c)].astype(jnp.float32)

    def core_copy(j, which):
        yy, xx = spots(which)
        return remote(
            g_ref.at[number(level(j), yy, xx, 1 - c)],
            core_b.at[j, which],
            core_s.at[j, which],
            core_r.at[j, which],
            to_core,
        )

    def diag_copy(j, which):
        part = (top, low)[which]
        return remote(
            acc.at[j, 3, part],
            diag_b.at[j, part],
            diag_s.at[j, which],
            diag_r.at[j, which],
            (to_x, to_y)[which],
        )

    def side_copy(j, which):
        return remote(
            acc.at[j, 1 + which],
            (y_b, x_b)[which].at[j],
            side_s.at[j, which],
            side_r.at[j, which],
            (to_y, to_x)[which],
        )

    def line_slot(side, step):
        return step if side == 1 else 3 + step

    def line_copy(j):
        side, step = order[j]
        slot = line_slot(side, step - 1)
        return remote(
            acc.at[j, 0],
            line_b.at[slot],
            line_s.at[j],
            line_r.at[slot],
            number(z + side, y, x, c),
        )

    def line_take(side, step):
        slot = line_slot(side, step)
        remote(
            acc.at[0, 0], line_b.at[slot], line_s.at[0], line_r.at[slot], number(z - side, y, x, c)
        ).wait_recv()
        out_ref[...] += line_b[slot].astype(jnp.float32)

    for which in (3, 1, 2, 0):
        for j in range(count):

            @pl.when(present(j))
            def _(j=j, which=which):
                core_copy(j, which).start()

    def first(j):
        @pl.when(present(j))
        def _():
            core_copy(j, 3).wait_recv()
            total = own_term(j, 3) + core_b[j, 3].astype(jnp.float32)
            acc[j, 3] = total.astype(jnp.bfloat16)
            diag_copy(j, 0).start()
            diag_copy(j, 1).start()

    def second(j):
        @pl.when(present(j))
        def _():
            core_copy(j, 1).wait_recv()
            diag_copy(j, 0).wait_recv()
            total = own_term(j, 1) + core_b[j, 1].astype(jnp.float32)
            acc[j, 1, top] = (total[:HALF] + diag_b[j, top].astype(jnp.float32)).astype(jnp.bfloat16)
            acc[j, 1, low] = total[HALF:].astype(jnp.bfloat16)
            side_copy(j, 0).start()
            core_copy(j, 2).wait_recv()
            diag_copy(j, 1).wait_recv()
            total = own_term(j, 2) + core_b[j, 2].astype(jnp.float32)
            acc[j, 2, top] = total[:HALF].astype(jnp.bfloat16)
            acc[j, 2, low] = (total[HALF:] + diag_b[j, low].astype(jnp.float32)).astype(jnp.bfloat16)
            side_copy(j, 1).start()

    def third(j):
        side, step = order[j]

        @pl.when(present(j))
        def _():
            core_copy(j, 0).wait_recv()
            side_copy(j, 0).wait_recv()
            side_copy(j, 1).wait_recv()
            out_ref[...] = (
                own_term(j, 0)
                + core_b[j, 0].astype(jnp.float32)
                + y_b[j].astype(jnp.float32)
                + x_b[j].astype(jnp.float32)
            )
            if side >= 0:

                @pl.when(z > 0)
                def _():
                    line_take(1, step)

            if side <= 0:

                @pl.when(z < 3)
                def _():
                    line_take(-1, step)

            if step:
                acc[j, 0] = out_ref[...].astype(jnp.bfloat16)
                line_copy(j).start()

    for t in range(count + 4):
        if t < count:
            first(t)
        if 0 <= t - 2 < count:
            second(t - 2)
        if 0 <= t - 4 < count:
            third(t - 4)
    start = 0
    for ref, each in zip((ada_ref, qkv_ref, wo_ref, up_ref, down_ref), COUNTS_PER_ROW):
        for i in range(12):
            ref[i * each : (i + 1) * each, :] = out_ref[
                i * SLOT + start : i * SLOT + start + each, :
            ]
        start += each
    bias_ref[...] = out_ref[start : start + 2, :]
    for j in range(count):

        @pl.when(present(j))
        def _(j=j):
            for which in range(4):
                core_copy(j, which).wait_send()
            for which in range(2):
                diag_copy(j, which).wait_send()
                side_copy(j, which).wait_send()
            if order[j][1]:
                line_copy(j).wait_send()


def scatter_sum(parts):
    sems = pltpu.SemaphoreType.DMA
    count = len(LINE)
    share = (ROWS, LANE)
    return pl.pallas_call(
        scatter_kernel,
        out_shape=[
            jax.ShapeDtypeStruct((rows, LANE), jnp.float32)
            for rows in [12 * each for each in COUNTS_PER_ROW] + [2]
        ],
        in_specs=[pl.BlockSpec(memory_space=pltpu.VMEM)],
        out_specs=[pl.BlockSpec(memory_space=pltpu.VMEM)] * 6,
        scratch_shapes=[
            pltpu.VMEM(share, jnp.float32),
            pltpu.VMEM((count, 4) + share, jnp.bfloat16),
            pltpu.VMEM((count, 4) + share, jnp.bfloat16),
            pltpu.VMEM((count,) + share, jnp.bfloat16),
            pltpu.VMEM((count,) + share, jnp.bfloat16),
            pltpu.VMEM((count,) + share, jnp.bfloat16),
            pltpu.VMEM((6,) + share, jnp.bfloat16),
            sems((count, 4)),
            sems((count, 4)),
            sems((count, 2)),
            sems((count, 2)),
            sems((count, 2)),
            sems((count, 2)),
            sems((count,)),
            sems((6,)),
        ],
        compiler_params=pltpu.CompilerParams(collective_id=2, has_side_effects=True),
        name="scatter_gradients",
    )(parts)


PAD = 16
TOK = 256
STARTS = (0, 18, 27, 30, 42)
BIAS_AT = (0, 2304, 2688, 3072, 3456, 4992)


def mm(left, right):
    return jnp.dot(left, right, preferred_element_type=jnp.float32)


def mm_back(left, right):
    return lax.dot_general(
        left, right, (((1,), (1,)), ((), ())), preferred_element_type=jnp.float32
    )


def mm_grad(left, right):
    return lax.dot_general(
        left, right, (((0,), (0,)), ((), ())), preferred_element_type=jnp.float32
    )


def block_kernel(
    x_ref, cond_ref, cot_ref, live_ref, bias_ref, all_ref,
    y_ref, gx_ref, gcond_ref, parts_ref, gbias_ref,
    flat, w_ada, w_qkv, w_out, w_up, w_down, down_f,
    mod, gmod, a1_s, qkv_s, prob_s, att_s, a2_s, act_s, slope_s,
    gm_s, gpre_s, gatt_s, gproj_s, n1_s, n2_s, r1_s, ao_s, mlp_s,
):
    rows = SLOT * 12
    bf, f32 = jnp.bfloat16, jnp.float32

    def widen(d, _):
        flat[pl.ds(pl.multiple_of(d * rows, 8), rows), :] = all_ref[d].astype(f32)
        return 0

    lax.fori_loop(0, 32, widen, 0)
    for ref, start, blocks in ((w_ada, 0, 18), (w_qkv, 18, 9), (w_out, 27, 3), (w_up, 30, 12)):
        for b in range(blocks):
            ref[:, b * 128 : (b + 1) * 128] = flat[pl.ds(start + b, D, stride=SLOT), :].astype(bf)
    for q in range(4):
        for b in range(3):
            down_f[b, pl.ds(q, D, stride=4), :] = flat[pl.ds(42 + 3 * q + b, D, stride=SLOT), :]
    for b in range(3):
        w_down[:, b * 128 : (b + 1) * 128] = down_f[b].astype(bf)

    cond = cond_ref[...].astype(f32)
    sigma = jax.nn.sigmoid(cond)
    c_act = (cond * sigma).astype(bf)
    for k in range(6):
        cols = slice(k * D, (k + 1) * D)
        mod[:, cols] = mm(c_act, w_ada[:, cols]) + bias_ref[:, cols]
    gmod[...] = jnp.zeros_like(gmod)
    gbias_ref[...] = jnp.zeros_like(gbias_ref)
    lane = lax.broadcasted_iota(jnp.int32, (TOK, 128), 1)
    masks = (lane < 64, lane >= 64)
    zero = jnp.zeros((TOK, 128), bf)

    def half(value, side):
        return jnp.where(masks[side], value, zero)

    def latent(l, _):
        tok = pl.ds(pl.multiple_of(l * TOK, TOK), TOK)
        row = pl.ds(l, 1)
        shift1, scale1, gate1, shift2, scale2, gate2 = [
            mod[row, k * D : (k + 1) * D] for k in range(6)
        ]
        live = live_ref[row, :]

        def bias(k, width=D, at=0):
            return bias_ref[:, BIAS_AT[k] + at : BIAS_AT[k] + at + width]

        def add_bias(k, value, at=0):
            width = value.shape[-1]
            spot_ = slice(BIAS_AT[k] + at, BIAS_AT[k] + at + width)
            gbias_ref[:, spot_] += jnp.sum(value, axis=0, keepdims=True)

        def put_mod(k, value):
            gmod[row, k * D : (k + 1) * D] = jnp.sum(value, axis=0, keepdims=True)

        resid = x_ref[tok, :].astype(f32)
        n1, inv1 = layer_norm(resid)
        n1_s[...] = n1
        a1_s[tok, :] = (n1 * (1.0 + scale1) + shift1).astype(bf)
        a1 = a1_s[tok, :]
        qkv_s[:, :D] = (mm(a1, w_qkv[:, :D]) + bias(1)).astype(bf)
        qkv_s[:, D : 2 * D] = mm(a1, w_qkv[:, D : 2 * D]).astype(bf)
        qkv_s[:, 2 * D :] = (mm(a1, w_qkv[:, 2 * D :]) + bias(2)).astype(bf)
        for pair in range(3):
            cols = slice(pair * 128, (pair + 1) * 128)
            q = qkv_s[:, pair * 128 : (pair + 1) * 128]
            k = qkv_s[:, D + pair * 128 : D + (pair + 1) * 128]
            v = qkv_s[:, 2 * D + pair * 128 : 2 * D + (pair + 1) * 128]
            total = None
            for side in range(2):
                scores = mm_back(half(q, side), k) * 0.125
                expd = jnp.exp(scores - jnp.max(scores, axis=-1, keepdims=True))
                probs = expd / jnp.sum(expd, axis=-1, keepdims=True)
                prob_s[2 * pair + side] = probs
                term = mm(probs.astype(bf), half(v, side))
                total = term if total is None else total + term
            att_s[tok, cols] = total.astype(bf)
        att_out = mm(att_s[tok, :], w_out[...]) + bias(3)
        ao_s[...] = att_out
        r1 = resid + gate1 * att_out
        r1_s[...] = r1
        n2, inv2 = layer_norm(r1)
        n2_s[...] = n2
        a2_s[tok, :] = (n2 * (1.0 + scale2) + shift2).astype(bf)
        a2 = a2_s[tok, :]
        for j in range(4):
            cols = slice(j * D, (j + 1) * D)
            pre = mm(a2, w_up[:, cols]) + bias(4, at=j * D)
            tangent = jnp.tanh(GELU_C * (pre + 0.044715 * pre * pre * pre))
            act_s[tok, cols] = (0.5 * pre * (1.0 + tangent)).astype(bf)
            slope_s[:, cols] = 0.5 * (1.0 + tangent) + 0.5 * pre * (
                1.0 - tangent * tangent
            ) * GELU_C * (1.0 + 3.0 * 0.044715 * pre * pre)
        mlp = mm(act_s[tok, :], w_down[...]) + bias(5)
        y_ref[tok, :] = (r1_s[...] + gate2 * mlp) * live

        gy = cot_ref[tok, :].astype(f32) * live
        put_mod(5, gy * mlp)
        gm = gy * gate2
        gm_s[tok, :] = gm.astype(bf)
        add_bias(5, gm)
        gm_b = gm_s[tok, :]
        for j in range(4):
            cols = slice(j * D, (j + 1) * D)
            gpre = mm_back(gm_b, w_down[cols, :]) * slope_s[:, cols]
            gpre_s[tok, cols] = gpre.astype(bf)
            add_bias(4, gpre, at=j * D)
        ga2 = mm_back(gpre_s[tok, :], w_up[...])
        n2 = n2_s[...]
        put_mod(4, ga2 * n2)
        put_mod(3, ga2)
        gy = cot_ref[tok, :].astype(f32) * live
        gr1 = gy + norm_backward(ga2 * (1.0 + scale2), n2, inv2)
        r1_s[...] = gr1
        put_mod(2, gr1 * ao_s[...])
        gatt = gr1 * gate1
        add_bias(3, gatt)
        gatt_s[tok, :] = gatt.astype(bf)
        gat = mm_back(gatt_s[tok, :], w_out[...]).astype(bf)
        for pair in range(3):
            cols = slice(pair * 128, (pair + 1) * 128)
            q = qkv_s[:, pair * 128 : (pair + 1) * 128]
            k = qkv_s[:, D + pair * 128 : D + (pair + 1) * 128]
            v = qkv_s[:, 2 * D + pair * 128 : 2 * D + (pair + 1) * 128]
            g = gat[:, cols]
            product = g.astype(f32) * att_s[tok, cols].astype(f32)
            gq = gk = gv = None
            for side in range(2):
                probs = prob_s[2 * pair + side]
                g_side = half(g, side)
                rowdot = jnp.sum(
                    jnp.where(masks[side], product, 0.0), axis=-1, keepdims=True
                )
                gs = (probs * (mm_back(g_side, v) - rowdot) * 0.125).astype(bf)
                tv = mm_grad(probs.astype(bf), g_side)
                tq = mm(gs, half(k, side))
                tk = mm_grad(gs, half(q, side))
                gv = tv if gv is None else gv + tv
                gq = tq if gq is None else gq + tq
                gk = tk if gk is None else gk + tk
            add_bias(1, gq, at=pair * 128)
            add_bias(2, gv, at=pair * 128)
            gproj_s[tok, cols] = gq.astype(bf)
            gproj_s[tok, D + pair * 128 : D + (pair + 1) * 128] = gk.astype(bf)
            gproj_s[tok, 2 * D + pair * 128 : 2 * D + (pair + 1) * 128] = gv.astype(bf)
        ga1 = mm_back(gproj_s[tok, :], w_qkv[...])
        n1 = n1_s[...]
        put_mod(1, ga1 * n1)
        put_mod(0, ga1)
        gx_ref[tok, :] = r1_s[...] + norm_backward(ga1 * (1.0 + scale1), n1, inv1)
        return 0

    lax.fori_loop(0, 2, latent, 0)

    for j in range(4):
        cols = slice(j * D, (j + 1) * D)
        grad = mm_grad(act_s[:, cols], gm_s[...])
        for b in range(3):
            down_f[b, cols, :] = grad[:, b * 128 : (b + 1) * 128]
    for q in range(4):
        for b in range(3):
            flat[pl.ds(42 + 3 * q + b, D, stride=SLOT), :] = down_f[b, pl.ds(q, D, stride=4), :]

    def put(start, left, right):
        for j in range(right.shape[-1] // D):
            grad = mm_grad(left, right[:, j * D : (j + 1) * D])
            for b in range(3):
                flat[pl.ds(start + 3 * j + b, D, stride=SLOT), :] = grad[
                    :, b * 128 : (b + 1) * 128
                ]

    put(30, a2_s[...], gpre_s)
    put(27, att_s[...], gatt_s)
    put(18, a1_s[...], gproj_s)
    gmod_b = gmod[...].astype(bf)
    gbias_ref[:, : 6 * D] = jnp.sum(gmod[...], axis=0, keepdims=True)
    for j in range(6):
        grad = mm_grad(c_act, gmod_b[:, j * D : (j + 1) * D])
        for b in range(3):
            flat[pl.ds(3 * j + b, D, stride=SLOT), :] = grad[:, b * 128 : (b + 1) * 128]
    gcond_ref[...] = mm_back(gmod_b, w_ada[...]) * (sigma * (1.0 + cond * (1.0 - sigma)))

    def narrow(d, _):
        parts_ref[d] = flat[pl.ds(pl.multiple_of(d * rows, 8), rows), :].astype(bf)
        return 0

    lax.fori_loop(0, 32, narrow, 0)


def block_call(inputs, cond, cotan, live, bias_all, everything):
    latents, tokens, width = inputs.shape
    n = latents * tokens
    bf, f32 = jnp.bfloat16, jnp.float32
    cond_pad = jnp.pad(cond, ((0, PAD - latents), (0, 0)))
    live_pad = jnp.broadcast_to(jnp.pad(live, (0, PAD - latents))[:, None], (PAD, width))
    bias_f = bias_all.astype(f32)[None, :]
    shape = jax.ShapeDtypeStruct
    v = pltpu.VMEM
    vmem = pl.BlockSpec(memory_space=pltpu.VMEM)
    y, gx, gcond, parts, gbias = pl.pallas_call(
        block_kernel,
        out_shape=[
            shape((n, width), f32),
            shape((n, width), f32),
            shape((PAD, width), f32),
            shape(everything.shape, bf),
            shape(bias_f.shape, f32),
        ],
        in_specs=[vmem] * 6,
        out_specs=[vmem] * 5,
        scratch_shapes=[
            v((32 * 12 * SLOT, 128), f32),
            v((D, 6 * D), bf),
            v((D, 3 * D), bf),
            v((D, D), bf),
            v((D, FF), bf),
            v((FF, D), bf),
            v((3, FF, 128), f32),
            v((PAD, 6 * D), f32),
            v((PAD, 6 * D), f32),
            v((n, D), bf),
            v((TOK, 3 * D), bf),
            v((HEADS, TOK, TOK), f32),
            v((n, D), bf),
            v((n, D), bf),
            v((n, FF), bf),
            v((TOK, FF), f32),
            v((n, D), bf),
            v((n, FF), bf),
            v((n, D), bf),
            v((n, 3 * D), bf),
            v((TOK, D), f32),
            v((TOK, D), f32),
            v((TOK, D), f32),
            v((TOK, D), f32),
            v((TOK, D), f32),
        ],
        compiler_params=pltpu.CompilerParams(vmem_limit_bytes=63 * 1024 * 1024),
        name="block_both_ways",
    )(inputs.reshape(n, width), cond_pad, cotan.reshape(n, width), live_pad, bias_f, everything)
    return (
        y.reshape(inputs.shape),
        gx.reshape(inputs.shape),
        gcond[:latents],
        parts,
        gbias.reshape(-1),
    )


def packed(weights):
    bias = jnp.pad(weights[5], (0, 2 * LANE - weights[5].shape[0]))
    return [w.reshape(-1, LANE) for w in (*weights[:5], bias)]


def shards(devices, inputs, cond, cotan, counts, *weights):
    latents, tokens, width = inputs.shape
    live = (jnp.arange(latents) < counts[0]).astype(jnp.float32)
    if devices == 32 and (latents, tokens, width) == (2, TOK, D):
        share = weights[5].shape[0]
        everything = gather_all(*packed(weights))
        bias_all = everything[:, 54:56].reshape(devices, 256)[:, :share].reshape(-1)
        output, g_inputs, g_cond, parts, g_bias = block_call(
            inputs, cond, cotan, live, bias_all, everything
        )
        g_bias = jnp.pad(g_bias.reshape(devices, share), ((0, 0), (0, 256 - share)))
        g_bias = g_bias.astype(jnp.bfloat16).reshape(devices, 2, 128)
        parts = lax.dynamic_update_slice(parts, g_bias, (0, 54, 0))
        shares = [block.reshape(-1) for block in scatter_sum(parts)]
        shares[5] = shares[5][:share]
        return (output, g_inputs, g_cond, *shares)
    gathered = [lax.all_gather(w, "dev", axis=0, tiled=True) for w in weights]
    mats = shape_weights(gathered)
    output, saved = device_forward(inputs, cond, live, mats)
    g_inputs, g_cond, grads = device_backward(cotan, live, mats, saved)
    shares = [lax.psum_scatter(g, "dev", scatter_dimension=0, tiled=True) for g in grads]
    return (output, g_inputs, g_cond, *shares)


def solution(mesh):
    in_specs = (
        P("dev", None, None),
        P("dev", None),
        P("dev", None, None),
        P("dev"),
        P("dev"),
        P("dev"),
        P("dev"),
        P("dev"),
        P("dev"),
        P("dev"),
    )
    out_specs = (
        P("dev", None, None),
        P("dev", None, None),
        P("dev", None),
        P("dev"),
        P("dev"),
        P("dev"),
        P("dev"),
        P("dev"),
        P("dev"),
    )
    return jax.shard_map(functools.partial(shards, mesh.shape["dev"]), mesh=mesh, in_specs=in_specs, out_specs=out_specs, check_vma=False)
```
